256 devices in a mesh: hit: 16 (over z, core), head: 16 (over x, y).
Axes of the slice: x: 4, y: 4, z: 8, core: 2. Of those that a mesh axis runs over, the one named last changes fastest.
Arguments:
- slots: bfloat16 [1024, 1024], replicated, may hold values from -700 to 700
- hits: bfloat16 [131072, 1024], P(('hit', 'head')), may hold values from -15 to 15
- hit_mask: int32 [131072], P('hit'), may hold values from 0 to 1, as said below
- q_weight: bfloat16 [1024, 1024], P(None, 'head'), may hold values from -0.1875 to 0.1875
- k_weight: bfloat16 [1024, 1024], replicated, may hold values from -0.1875 to 0.1875
- v_weight: bfloat16 [1024, 1024], replicated, may hold values from -0.1875 to 0.1875
- o_weight: bfloat16 [1024, 1024], P('head'), may hold values from -0.1875 to 0.1875
Outputs:
- attended: bfloat16 [1024, 1024], P('hit', 'head')
The draws below stay inside these ranges and needn't reach their ends.
Inputs may be any that keep to these rules, and one draw needn't show every extreme that they name: `hit_mask`: within each group of 8192 hits the real hits form a prefix of 2048 hits or more; in some group every hit is real.
All inputs are finite; a program needn't handle non-finite values.
Results may differ from the reference program's by a relative error of at most 0.0098.
Values may be sent and summed in bfloat16 or wider, within the bound.
A program may use at most 128 MiB of HBM per device.

```python
import jax
import jax.numpy as jnp
from jax import lax

D = 1024
HEADS = 16
HEAD_DIM = 64
SLOTS = 1024
GROUP = 8192
HITS = 131072


def draw_slots(key, part):
    first_key = jax.random.fold_in(key, 0)
    base = jnp.clip(jax.random.normal(first_key, (SLOTS, D), jnp.float32), -6.0, 6.0)
    return base.astype(jnp.bfloat16)


def draw_hit_mask(key, part):
    first_key, second_key = jax.random.split(key, 2)
    groups = HITS // GROUP
    lengths = jax.random.randint(first_key, (groups,), GROUP // 4, GROUP + 1)
    full_group = jax.random.randint(second_key, (), 0, groups)
    lengths = jnp.where(jnp.arange(groups) == full_group, GROUP, lengths)
    positions = jnp.arange(HITS) % GROUP
    owners = jnp.arange(HITS) // GROUP
    return (positions < lengths[owners]).astype(jnp.int32)


def block_levels(key, extent, pieces, low, high):
    def one(axis_at, parts):
        steps = jax.random.uniform(jax.random.fold_in(jax.random.fold_in(key, 6), axis_at), (parts,), jnp.float32, low / len(pieces), high / len(pieces))
        return jnp.repeat(jnp.exp(steps), extent[axis_at] // parts).reshape((-1,) + (1,) * (len(extent) - axis_at - 1))

    factor_of = one(*pieces[0])
    for cut in pieces[1:]:
        factor_of = factor_of * one(*cut)
    return factor_of


def centred(stream_key, dims, scale, limit, cuts=(), dtype=jnp.bfloat16):
    factor_of = block_levels(stream_key, dims, cuts, -0.22, 0.18) if cuts else 1.0
    drawn = jax.random.normal(stream_key, dims, jnp.float32) * scale * factor_of
    return jnp.minimum(jnp.maximum(drawn, -limit), limit).astype(dtype)


def setup_inputs(seed: int = 0) -> dict:
    arg_keys = jax.random.split(jax.random.key(seed), 8)
    return {
        "slots": draw_slots(jax.random.fold_in(arg_keys[7], 71), 0),
        "hits": centred(arg_keys[1], (HITS, D), 3.0, 15.0, ((0, 256),)),
        "hit_mask": draw_hit_mask(jax.random.fold_in(arg_keys[7], 71), 0),
        "q_weight": centred(arg_keys[3], (D, D), D ** -0.5, 0.1875, ((1, 16),)),
        "k_weight": centred(arg_keys[4], (D, D), D ** -0.5, 0.1875),
        "v_weight": centred(arg_keys[5], (D, D), D ** -0.5, 0.1875),
        "o_weight": centred(arg_keys[6], (D, D), D ** -0.5, 0.1875, ((0, 16),)),
    }


def attend(queries_head, keys_head, values_head, valid):
    scores = jnp.dot(queries_head, keys_head.T, preferred_element_type=jnp.float32) * (HEAD_DIM ** -0.5)
    scores = jnp.where(valid[None, :] > 0, scores, jnp.float32(-1e30))
    row_top = jnp.max(scores, axis=1)
    expo = jnp.exp(scores - row_top[:, None])
    totals = jnp.sum(expo, axis=1)
    weights = expo.astype(jnp.bfloat16)
    partial_value = jnp.dot(weights, values_head, preferred_element_type=jnp.float32)
    return row_top, totals, partial_value


def reference(slots, hits, hit_mask, q_weight, k_weight, v_weight, o_weight):
    queries = jnp.dot(slots, q_weight, preferred_element_type=jnp.float32).astype(jnp.bfloat16)
    queries = queries.reshape(SLOTS, HEADS, HEAD_DIM).transpose(1, 0, 2)
    groups = HITS // GROUP

    def group_part(inputs):
        group_rows, valid = inputs
        keys = jnp.dot(group_rows, k_weight, preferred_element_type=jnp.float32).astype(jnp.bfloat16)
        values = jnp.dot(group_rows, v_weight, preferred_element_type=jnp.float32).astype(jnp.bfloat16)
        keys = keys.reshape(GROUP, HEADS, HEAD_DIM).transpose(1, 0, 2)
        values = values.reshape(GROUP, HEADS, HEAD_DIM).transpose(1, 0, 2)

        def head_part(head_inputs):
            return attend(head_inputs[0], head_inputs[1], head_inputs[2], valid)

        return lax.map(head_part, (queries, keys, values))

    row_tops, totals, partials = lax.map(group_part, (hits.reshape(groups, GROUP, D), hit_mask.reshape(groups, GROUP)))
    overall = jnp.max(row_tops, axis=0)
    scale = jnp.exp(row_tops - overall[None])
    numer = jnp.sum(partials * scale[..., None], axis=0)
    denom = jnp.sum(totals * scale, axis=0)
    mixed = (numer / denom[..., None]).astype(jnp.bfloat16)
    mixed = mixed.transpose(1, 0, 2).reshape(SLOTS, D)
    return jnp.dot(mixed, o_weight, preferred_element_type=jnp.float32).astype(jnp.bfloat16)
```

```python
import functools

import jax
import jax.numpy as jnp
from jax import lax
from jax.experimental import pallas as pl
from jax.experimental.pallas import tpu as pltpu
from jax.sharding import PartitionSpec as P

MESH = pl.DeviceIdType.MESH
HEAD_DIM = 64
SIDE = 4
F32, BF16 = jnp.float32, jnp.bfloat16
MASKED = -1e30


def kernel(
    slots_hbm, hits_hbm, mask_ref, qw_hbm, kw_hbm, vw_hbm, ow_hbm, out_ref,
    slots_v, hits_v, qw_v, wbuf, sbuf, rbuf, qt, top, acc,
    zso, zsm, zro, zrm, mt, owall,
    ld, ldk, ldv, kv_ss, kv_rs, ow_ss, ow_rs, zo_ss, zo_rs, zm_ss, zm_rs, g_ss, g_rs,
):
    i = lax.axis_index("hit")
    h = lax.axis_index("head")
    x, y = h // SIDE, h % SIDE
    yy, c = y // 2, i % 2
    other = i + 1 - 2 * c

    barrier = pltpu.get_barrier_semaphore()

    def greet_head(j, carry):
        pl.semaphore_signal(
            barrier, inc=1, device_id={"hit": i, "head": lax.rem(h + j, 16)}, device_id_type=MESH
        )
        return carry

    def greet_other(j, carry):
        pl.semaphore_signal(
            barrier, inc=1, device_id={"hit": other, "head": j}, device_id_type=MESH
        )
        return carry

    def greet_hit(j, carry):
        step = lax.rem(i + j, 16)

        @pl.when(step != other)
        def _():
            pl.semaphore_signal(
                barrier, inc=1, device_id={"hit": step, "head": h}, device_id_type=MESH
            )

        return carry

    lax.fori_loop(1, 16, greet_head, 0)
    lax.fori_loop(0, 16, greet_other, 0)
    lax.fori_loop(1, 16, greet_hit, 0)

    def offsets(t):
        u = t // 2
        return (10 - u * (u + 1) // 2) % SIDE, 1 - t % 2

    def target_pair(t):
        dx, dyy = offsets(t)
        return ((x + dx) % SIDE) * 2 + (yy + dyy) % 2

    hits_cp = pltpu.make_async_copy(hits_hbm, hits_v, ld.at[0])
    slots_cp = pltpu.make_async_copy(slots_hbm, slots_v, ld.at[1])
    qw_cp = pltpu.make_async_copy(qw_hbm, qw_v, ld.at[2])

    def weights(t):
        cols = pl.ds(pl.multiple_of(target_pair(t) * 128, 128), 128)
        return (
            pltpu.make_async_copy(kw_hbm.at[:, cols], wbuf.at[t, :, pl.ds(0, 128)], ldk.at[t]),
            pltpu.make_async_copy(vw_hbm.at[:, cols], wbuf.at[t, :, pl.ds(128, 128)], ldv.at[t]),
        )

    def start_weights(t, carry):
        for cp in weights(t):
            cp.start()
        return carry

    hits_cp.start()
    lax.fori_loop(0, 2, start_weights, 0)
    slots_cp.start()
    qw_cp.start()
    lax.fori_loop(2, 8, start_weights, 0)

    lane = lax.broadcasted_iota(jnp.int32, (512, 128), 1)
    low = lane < HEAD_DIM

    def send_kv(head):
        return pltpu.make_async_remote_copy(
            src_ref=sbuf.at[head], dst_ref=rbuf.at[h],
            send_sem=kv_ss.at[head], recv_sem=kv_rs.at[h],
            device_id={"head": head}, device_id_type=MESH,
        )

    def recv_kv(head):
        return pltpu.make_async_remote_copy(
            src_ref=sbuf.at[head], dst_ref=rbuf.at[head],
            send_sem=kv_ss.at[head], recv_sem=kv_rs.at[head],
            device_id={"head": head}, device_id_type=MESH,
        )

    hits_cp.wait()

    def project(t, carry):
        for cp in weights(t):
            cp.wait()
        both = jnp.dot(hits_v[...], wbuf[t], preferred_element_type=F32)
        keys, values = both[:, :128], both[:, 128:]
        first = jnp.where(low, keys, pltpu.roll(values, 64, 1)).astype(BF16)
        second = jnp.where(low, pltpu.roll(keys, 64, 1), values).astype(BF16)
        base = target_pair(t) * 2

        @pl.when(t == 0)
        def _():
            pl.semaphore_wait(barrier, 45)

        for j, block in ((0, first), (1, second)):
            head = base + j
            sbuf[head] = block

            @pl.when(head != h)
            def _():
                send_kv(head).start()

        return carry

    lax.fori_loop(0, 8, project, 0)

    slots_cp.wait()
    qw_cp.wait()
    queries = jnp.dot(slots_v[...], qw_v[...], preferred_element_type=F32).astype(BF16)
    queries = queries.astype(F32) * HEAD_DIM ** -0.5
    wide = jnp.concatenate([queries, jnp.zeros((1024, 64), F32)], axis=1)
    qt[...] = wide.T.astype(BF16)

    def send_ow(head):
        cols = pl.ds(pl.multiple_of((head // 2) * 128, 128), 128)
        rows = pl.ds(pl.multiple_of(h * 64, 64), 64)
        return pltpu.make_async_remote_copy(
            src_ref=ow_hbm.at[:, cols], dst_ref=owall.at[rows, :],
            send_sem=ow_ss.at[head], recv_sem=ow_rs.at[h],
            device_id={"head": head}, device_id_type=MESH,
        )

    def recv_ow(head):
        cols = pl.ds(0, 128)
        rows = pl.ds(pl.multiple_of(head * 64, 64), 64)
        return pltpu.make_async_remote_copy(
            src_ref=ow_hbm.at[:, cols], dst_ref=owall.at[rows, :],
            send_sem=ow_ss.at[head], recv_sem=ow_rs.at[head],
            device_id={"head": head}, device_id_type=MESH,
        )

    def start_ow(j, carry):
        send_ow(lax.rem(h + j, 16)).start()
        return carry

    lax.fori_loop(1, 16, start_ow, 0)
    own_cols = pl.ds(pl.multiple_of((h // 2) * 128, 128), 128)
    own_rows = pl.ds(pl.multiple_of(h * 64, 64), 64)
    own_ow = pltpu.make_async_copy(ow_hbm.at[:, own_cols], owall.at[own_rows, :], ld.at[3])
    own_ow.start()

    count = jnp.sum(mask_ref[...].astype(F32), keepdims=True)
    rowid = lax.broadcasted_iota(jnp.int32, (512, 1), 0)
    top[...] = jnp.full(top.shape, MASKED, F32)
    acc[...] = jnp.zeros(acc.shape, F32)

    def attend(kv, head):
        position = (rowid + head * 512).astype(F32)
        bias = jnp.where(position < count, 0.0, MASKED)
        vxt = jnp.where(low, jnp.ones_like(kv), kv).T
        for b in range(4):
            cols = slice(256 * b, 256 * b + 256)
            s = jnp.dot(kv, qt[:, cols], preferred_element_type=F32) + bias
            before = top[:, cols]
            now = jnp.maximum(before, jnp.max(s, axis=0, keepdims=True))
            p = jnp.exp(s - now).astype(BF16)
            acc[:, cols] = acc[:, cols] * jnp.exp(before - now) + jnp.dot(
                vxt, p, preferred_element_type=F32
            )
            top[:, cols] = now

    attend(sbuf[h], h)

    def chunk(q, carry):
        dx, dyy = offsets(q // 2)
        source = ((x + SIDE - dx) % SIDE) * SIDE + ((yy + dyy) % 2) * 2 + q % 2

        @pl.when(source != h)
        def _():
            recv_kv(source).wait_recv()
            attend(rbuf[source], source)

        return carry

    lax.fori_loop(0, 16, chunk, 0)

    for z in range(8):
        cols = slice(128 * z, 128 * z + 128)
        zso[z] = acc[64:, cols].astype(BF16)
        zsm[z, 0:1] = top[:, cols]
        zsm[z, 1:2] = acc[0:1, cols]

    def z_copy(to, src, slot):
        half = pl.ds(pl.multiple_of((src % 2) * 32, 32), 32)
        return (
            pltpu.make_async_remote_copy(
                src_ref=zso.at[src // 2, half, :], dst_ref=zro.at[slot],
                send_sem=zo_ss.at[src], recv_sem=zo_rs.at[slot],
                device_id={"hit": to}, device_id_type=MESH,
            ),
            pltpu.make_async_remote_copy(
                src_ref=zsm.at[src // 2], dst_ref=zrm.at[slot],
                send_sem=zm_ss.at[src], recv_sem=zm_rs.at[slot],
                device_id={"hit": to}, device_id_type=MESH,
            ),
        )

    def z_send(j, carry):
        to = lax.rem(i + 4 + j, 16)

        @pl.when(to != i)
        def _():
            for cp in z_copy(to, to, i):
                cp.start()

        return carry

    lax.fori_loop(0, 16, z_send, 0)
    my_half = pl.ds(pl.multiple_of(c * 32, 32), 32)
    zro[i] = zso[i // 2, my_half, :]
    zrm[i] = zsm[i // 2]

    def z_wait(j, carry):
        to = lax.rem(i + j, 16)
        for cp in z_copy(to, to, to):
            cp.wait_recv()
        return carry

    lax.fori_loop(1, 16, z_wait, 0)
    tops = zrm[:, 0:1, :]
    sums = zrm[:, 1:2, :]
    scale = jnp.exp(tops - jnp.max(tops, axis=0, keepdims=True))
    denom = jnp.sum(sums * scale, axis=0)
    numer = jnp.sum(zro[...].astype(F32) * scale, axis=0)
    mine = pl.ds(pl.multiple_of(h * 64 + c * 32, 32), 32)
    mt[mine, :] = (numer / denom).astype(BF16)

    def g_copy(hit, head, rows, s_sem, r_sem):
        return pltpu.make_async_remote_copy(
            src_ref=mt.at[rows, :], dst_ref=mt.at[rows, :],
            send_sem=g_ss.at[s_sem], recv_sem=g_rs.at[r_sem],
            device_id={"hit": hit, "head": head}, device_id_type=MESH,
        )

    me = 2 * h + c

    def g_send(j, carry):
        peer = lax.rem(me + j, 32)
        g_copy(i - c + peer % 2, peer // 2, mine, peer, me).start()
        return carry

    lax.fori_loop(1, 32, g_send, 0)

    def o_wait(j, carry):
        recv_ow(lax.rem(h + j, 16)).wait_recv()
        return carry

    lax.fori_loop(1, 16, o_wait, 0)
    own_ow.wait()

    def g_wait(j, carry):
        peer = lax.rem(me + j, 32)
        rows = pl.ds(pl.multiple_of(peer * 32, 32), 32)
        g_copy(i - c + peer % 2, peer // 2, rows, peer, peer).wait_recv()
        return carry

    lax.fori_loop(1, 32, g_wait, 0)
    full = jnp.dot(mt[...].T, owall[...], preferred_element_type=F32)
    rows_here = jnp.where(c == 0, full[:64], full[64:])
    out_ref[...] = jnp.where(h % 2 == 0, rows_here[:, :64], rows_here[:, 64:]).astype(BF16)

    def drain_head(j, carry):
        head = lax.rem(h + j, 16)
        send_kv(head).wait_send()
        send_ow(head).wait_send()
        to = lax.rem(i + j, 16)
        for cp in z_copy(to, to, to):
            cp.wait_send()
        return carry

    lax.fori_loop(1, 16, drain_head, 0)

    def drain_g(j, carry):
        peer = lax.rem(me + j, 32)
        g_copy(i - c + peer % 2, peer // 2, mine, peer, peer).wait_send()
        return carry

    lax.fori_loop(1, 32, drain_g, 0)


def local(slots, hits, hit_mask, q_weight, k_weight, v_weight, o_weight):
    anywhere = pl.BlockSpec(memory_space=pl.ANY)
    vmem = pl.BlockSpec(memory_space=pltpu.VMEM)
    dma = pltpu.SemaphoreType.DMA
    return pl.pallas_call(
        kernel,
        out_shape=jax.ShapeDtypeStruct((64, 64), BF16),
        in_specs=[anywhere, anywhere, vmem, anywhere, anywhere, anywhere, anywhere],
        out_specs=vmem,
        scratch_shapes=[
            pltpu.VMEM((1024, 1024), BF16),
            pltpu.VMEM((512, 1024), BF16),
            pltpu.VMEM((1024, 64), BF16),
            pltpu.VMEM((8, 1024, 256), BF16),
            pltpu.VMEM((16, 512, 128), BF16),
            pltpu.VMEM((16, 512, 128), BF16),
            pltpu.VMEM((128, 1024), BF16),
            pltpu.VMEM((1, 1024), F32),
            pltpu.VMEM((128, 1024), F32),
            pltpu.VMEM((8, 64, 128), BF16),
            pltpu.VMEM((8, 8, 128), F32),
            pltpu.VMEM((16, 32, 128), BF16),
            pltpu.VMEM((16, 8, 128), F32),
            pltpu.VMEM((1024, 128), BF16),
            pltpu.VMEM((1024, 128), BF16),
            dma((4,)), dma((8,)), dma((8,)),
            dma((16,)), dma((16,)), dma((16,)), dma((16,)),
            dma((16,)), dma((16,)), dma((16,)), dma((16,)),
            dma((32,)), dma((32,)),
        ],
        compiler_params=pltpu.CompilerParams(
            collective_id=0, has_side_effects=True, vmem_limit_bytes=48 << 20
        ),
    )(slots, hits, hit_mask.reshape(64, 128), q_weight, k_weight, v_weight, o_weight)


def solution(mesh):
    placed = (P(), P(("hit", "head"), None), P("hit"), P(None, "head"), P(), P(), P("head", None))
    return jax.shard_map(
        local, mesh=mesh, in_specs=placed, out_specs=P("hit", "head"), check_vma=False
    )
```
